256 devices in a mesh: dp: 16 (over z, core), tensor: 16 (over x, y).
Axes of the slice: x: 4, y: 4, z: 8, core: 2. Of those that a mesh axis runs over, the one named last changes fastest.
Arguments:
- inputs: bfloat16 [4096, 6144], P('dp'), may hold values from -6 to 6
- grad_hidden: bfloat16 [4096, 24576], P('dp', 'tensor'), may hold values from -6 to 6
- w_blocks: bfloat16 [16, 288, 128, 128], P('tensor', 'dp'), may hold values from -0.15625 to 0.15625
- block_ids: int32 [16, 288], P('tensor', 'dp'), may hold values from 0 to 575, as said below
- counts: int32 [16, 16], P('tensor', 'dp'), may hold values from 1 to 18, 144 in all within a row
Outputs:
- hidden: bfloat16 [4096, 24576], P('dp', 'tensor')
- grad_inputs: bfloat16 [4096, 6144], P('dp', 'tensor')
- grad_blocks: bfloat16 [16, 288, 128, 128], P('tensor', 'dp')
The draws below stay inside these ranges and needn't reach their ends.
Inputs may be any that keep to these rules, and one draw needn't show every extreme that they name: `block_ids`: within one tensor index all 288 ids are distinct. Each row of counts sums to 144.
All inputs are finite; a program needn't handle non-finite values. No bound on the sum of `counts` on one device may be relied on, other than what follows from the above.
Results may differ from the reference program's by a relative error of at most 0.023.
Values may be sent and summed in bfloat16 or wider, within the bound.
A program may use at most 128 MiB of HBM per device.

```python
import math
import jax
import jax.numpy as jnp
import numpy as np
from jax import lax

D = 6144
FF = 24576
BLK = 128
TOK_DEV = 256
TOKENS = 4096
FF_DEV = 1536
RB = 48
CB = 12
NBLK = 576
NNZ = 144
CAP = 18
SLOTS = 288
N_DP = 16
N_TENSOR = 16


def draw_block_ids(key, part):
    row_keys = jax.random.split(key, N_TENSOR)

    def one_row(row_key):
        return jax.random.permutation(row_key, NBLK)[:SLOTS]
    return jax.vmap(one_row)(row_keys).astype(jnp.int32)


def level_of(stream_key, extent, cuts, smallest, high):
    gain, own = 1.0, jax.random.fold_in(stream_key, 6)
    for dim, parts in cuts:
        steps = jnp.exp(jax.random.uniform(jax.random.fold_in(own, dim), (parts,), jnp.float32, smallest / len(cuts), high / len(cuts)))
        gain = gain * jnp.repeat(steps, extent[dim] // parts).reshape([-1 if axis == dim else 1 for axis in range(len(extent))])
    return gain


def length_profile(count, total, limit, lean):
    weights = [(1 << 20) // math.isqrt(rank ** lean) + 1 for rank in range(2, count + 1)]
    surplus, given = total - limit - (count - 1), [1] * (count - 1)
    while surplus > 0:
        candidates = [i for i in range(count - 1) if given[i] < limit]
        pool, remaining = sum([weights[i] for i in candidates]), surplus
        for i in candidates:
            addition = min(limit - given[i], max(1, remaining * weights[i] // pool), surplus)
            given[i] = given[i] + addition
            surplus = surplus - addition
    return np.array([limit] + given)


def uneven_parts(key, count, total, most, lean):
    if count == 2:
        one = jax.random.randint(key, (), max(1, total - most), min(most, total - 1) + 1)
        return jnp.stack([one, total - one])
    tallies = jnp.asarray(length_profile(count, total, most, lean), jnp.int32)
    pairs = (count - 1) // 2
    source_of, sink = tallies[1:1 + 2 * pairs:2], tallies[2:2 + 2 * pairs:2]
    margin = jnp.minimum(source_of - 1, most - sink)
    shifted = jax.random.randint(jax.random.fold_in(key, 1), (pairs,), 0, 1 << 20) % (margin + 1)
    tallies = tallies.at[1:1 + 2 * pairs:2].set(source_of - shifted).at[2:2 + 2 * pairs:2].set(sink + shifted)
    return tallies[jax.random.permutation(jax.random.fold_in(key, 2), count)]


def gaussian(stream_key, extent, spread, limit, cuts=(), kind=jnp.bfloat16):
    gain = level_of(stream_key, extent, cuts, -0.22, 0.18) if cuts else 1.0
    entries = jax.random.normal(stream_key, extent, jnp.float32) * spread * gain
    return jnp.minimum(jnp.maximum(entries, -limit), limit).astype(kind)


def setup_inputs(seed: int = 0) -> dict:
    arg_keys = jax.random.split(jax.random.key(seed), 6)
    return {
        "inputs": gaussian(arg_keys[0], (TOKENS, D), 1.0, 6.0, ((0, 16),)),
        "grad_hidden": gaussian(arg_keys[1], (TOKENS, FF), 1.0, 6.0, ((0, 16), (1, 16))),
        "w_blocks": gaussian(arg_keys[2], (N_TENSOR, SLOTS, BLK, BLK), (D // 4) ** -0.5, 0.15625, ((0, 16), (1, 16))),
        "block_ids": draw_block_ids(jax.random.fold_in(arg_keys[5], 71), 0),
        "counts": jax.vmap(lambda own: uneven_parts(own, N_DP, NNZ, CAP, 2))(jax.random.split(arg_keys[4], N_TENSOR)).reshape((N_TENSOR, N_DP)).astype(jnp.int32),
    }


GELU_C = 0.7978845608028654
GELU_A = 0.044715

def gelu_value(values):
    inner_arg = GELU_C * (values + GELU_A * values * values * values)
    return 0.5 * values * (1.0 + jnp.tanh(inner_arg))

def gelu_slope(values):
    inner_arg = GELU_C * (values + GELU_A * values * values * values)
    tanh_value = jnp.tanh(inner_arg)
    return 0.5 * (1.0 + tanh_value) + 0.5 * values * (1.0 - tanh_value * tanh_value) * GELU_C * (1.0 + 3.0 * GELU_A * values * values)

def shard_pass(x_blocks, x_groups, blocks, ids_row, owner_counts, grad_cols):
    slot_index = jnp.arange(SLOTS, dtype=jnp.int32)
    is_live = slot_index % CAP < owner_counts[slot_index // CAP]
    live_order = jnp.argsort(jnp.where(is_live, 0, 1).astype(jnp.int32), stable=True)[:NNZ].astype(jnp.int32)
    live_ids = ids_row[live_order].astype(jnp.int32)
    row_index = (live_ids // CB).astype(jnp.int32)
    col_index = (live_ids % CB).astype(jnp.int32)
    chosen = blocks[live_order].astype(jnp.float32)
    grouped = (chosen.reshape(NNZ // 16, 16, BLK, BLK), row_index.reshape(NNZ // 16, 16), col_index.reshape(NNZ // 16, 16))

    def forward_group(running, group_data):
        block_piece, rows_here, cols_here = group_data
        x_rows = x_blocks[:, rows_here, :].astype(jnp.float32)
        product = jnp.einsum('tgb,gbc->tgc', x_rows, block_piece, precision=lax.Precision.HIGHEST)
        return (running.at[:, cols_here, :].add(product), None)
    pre_three, unused = lax.scan(forward_group, jnp.zeros((TOKENS, CB, BLK), jnp.float32), grouped)
    pre_act = pre_three.reshape(TOKENS, FF_DEV)
    hidden = gelu_value(pre_act).astype(jnp.bfloat16)
    grad_pre = (grad_cols.astype(jnp.float32) * gelu_slope(pre_act)).astype(jnp.bfloat16)
    grad_three = grad_pre.reshape(TOKENS, CB, BLK)

    def backward_group(running, group_data):
        block_piece, rows_here, cols_here = group_data
        grad_piece = grad_three[:, cols_here, :].astype(jnp.float32)
        contrib = jnp.einsum('tgc,gbc->tgb', grad_piece, block_piece, precision=lax.Precision.HIGHEST)
        x_rows = x_groups[:, :, rows_here, :].astype(jnp.float32)
        group_grad = jnp.einsum('ntgb,ntgc->ngbc', x_rows, grad_piece.reshape(N_DP, TOK_DEV, 16, BLK), precision=lax.Precision.HIGHEST)
        group_grad = lax.optimization_barrier(group_grad.astype(jnp.bfloat16)).astype(jnp.float32)
        return (running.at[:, rows_here, :].add(contrib), lax.optimization_barrier(jnp.sum(group_grad, axis=0)))
    input_three, weight_parts = lax.scan(backward_group, jnp.zeros((TOKENS, RB, BLK), jnp.float32), grouped)
    partial_t = input_three.reshape(TOKENS, D).astype(jnp.bfloat16)
    summed = jnp.zeros((SLOTS, BLK, BLK), jnp.float32).at[live_order].set(weight_parts.reshape(NNZ, BLK, BLK))
    grad_blocks = (summed * (1.0 / math.sqrt(TOKENS))).astype(jnp.bfloat16)
    return (hidden, partial_t, grad_blocks)

def reference(inputs, grad_hidden, w_blocks, block_ids, counts):
    x_blocks = inputs.reshape(TOKENS, RB, BLK)
    x_groups = inputs.reshape(N_DP, TOK_DEV, RB, BLK)
    grad_shards = grad_hidden.reshape(TOKENS, N_TENSOR, FF_DEV).transpose(1, 0, 2)

    def one_shard(running, shard_data):
        blocks, ids_row, owner_counts, grad_cols = shard_data
        hidden, partial_t, grad_blocks = shard_pass(x_blocks, x_groups, blocks, ids_row, owner_counts, grad_cols)
        rounded = lax.optimization_barrier(partial_t).astype(jnp.float32)
        return (running + rounded, (hidden, grad_blocks))
    total, outputs = lax.scan(one_shard, jnp.zeros((TOKENS, D), jnp.float32), (w_blocks, block_ids, counts, grad_shards))
    hiddens, grad_blocks = outputs
    hidden = hiddens.transpose(1, 0, 2).reshape(TOKENS, FF)
    return (hidden, total.astype(jnp.bfloat16), grad_blocks)
```

```python
import functools
import math

import jax
import jax.numpy as jnp
from jax import lax
from jax.experimental import pallas as pl
from jax.experimental.pallas import tpu as pltpu
from jax.sharding import PartitionSpec as P

GELU_C = 0.7978845608028654
GELU_A = 0.044715


def gelu_value(values):
    inner_arg = GELU_C * (values + GELU_A * values * values * values)
    return 0.5 * values * (1.0 + jnp.tanh(inner_arg))


def gelu_slope(values):
    inner_arg = GELU_C * (values + GELU_A * values * values * values)
    tanh_value = jnp.tanh(inner_arg)
    return 0.5 * (1.0 + tanh_value) + 0.5 * values * (1.0 - tanh_value * tanh_value) * GELU_C * (
        1.0 + 3.0 * GELU_A * values * values
    )


def block_kernel(capacity, col_blocks, ids_ref, counts_ref, x_ref, gh_ref, w_ref,
                 hidden_ref, partial_ref, gg_ref, pre_ref, gp_ref, acc_ref):
    slots = w_ref.shape[0]
    blk = w_ref.shape[-1]

    def slot_info(s):
        live = (s % capacity) < counts_ref[s // capacity]
        bid = ids_ref[s]
        row = pl.multiple_of((bid // col_blocks) * blk, blk)
        col = pl.multiple_of((bid % col_blocks) * blk, blk)
        return live, row, col

    pre_ref[...] = jnp.zeros_like(pre_ref)

    def fwd(s, carry):
        live, row, col = slot_info(s)

        @pl.when(live)
        def _():
            xr = x_ref[:, pl.ds(row, blk)]
            prod = jnp.dot(xr, w_ref[s], preferred_element_type=jnp.float32)
            pre_ref[:, pl.ds(col, blk)] += prod

        return carry

    lax.fori_loop(0, slots, fwd, 0)

    pre = pre_ref[...]
    hidden_ref[...] = gelu_value(pre).astype(hidden_ref.dtype)
    gp_ref[...] = (gh_ref[...].astype(jnp.float32) * gelu_slope(pre)).astype(gp_ref.dtype)
    acc_ref[...] = jnp.zeros_like(acc_ref)

    def bwd(s, carry):
        live, row, col = slot_info(s)

        @pl.when(live)
        def _():
            g = gp_ref[:, pl.ds(col, blk)]
            w = w_ref[s]
            contrib = lax.dot_general(g, w, (((1,), (1,)), ((), ())),
                                      preferred_element_type=jnp.float32)
            acc_ref[:, pl.ds(row, blk)] += contrib
            xr = x_ref[:, pl.ds(row, blk)]
            part = lax.dot_general(xr, g, (((0,), (0,)), ((), ())),
                                   preferred_element_type=jnp.float32)
            gg_ref[s] = part.astype(gg_ref.dtype)

        @pl.when(jnp.logical_not(live))
        def _():
            gg_ref[s] = jnp.zeros((blk, blk), gg_ref.dtype)

        return carry

    lax.fori_loop(0, slots, bwd, 0)
    partial_ref[...] = acc_ref[...].astype(partial_ref.dtype)


def local_pass(x, gh, w, ids, counts, capacity, col_blocks):
    tok, width = x.shape
    ff = gh.shape[1]
    slots, blk, _ = w.shape
    smem = pl.BlockSpec(memory_space=pltpu.SMEM)
    vmem = pl.BlockSpec(memory_space=pltpu.VMEM)
    flops = 3 * 2 * tok * blk * blk * (slots // 2)
    bytes_accessed = 2 * (x.size + gh.size + 2 * w.size + tok * ff + tok * width)
    return pl.pallas_call(
        functools.partial(block_kernel, capacity, col_blocks),
        out_shape=(
            jax.ShapeDtypeStruct((tok, ff), jnp.bfloat16),
            jax.ShapeDtypeStruct((tok, width), jnp.bfloat16),
            jax.ShapeDtypeStruct((slots, blk, blk), jnp.bfloat16),
        ),
        in_specs=[smem, smem, vmem, vmem, vmem],
        out_specs=(vmem, vmem, vmem),
        scratch_shapes=[
            pltpu.VMEM((tok, ff), jnp.float32),
            pltpu.VMEM((tok, ff), jnp.bfloat16),
            pltpu.VMEM((tok, width), jnp.float32),
        ],
        compiler_params=pltpu.CompilerParams(vmem_limit_bytes=60 * 1024 * 1024),
        cost_estimate=pl.CostEstimate(flops=flops, transcendentals=tok * ff * 2,
                                      bytes_accessed=bytes_accessed),
    )(ids, counts, x, gh, w)


def per_device(inputs, grad_hidden, w_blocks, block_ids, counts):
    tok_rows, model_width = inputs.shape
    block_size = w_blocks.shape[-1]
    capacity = w_blocks.shape[1]
    col_blocks = grad_hidden.shape[1] // block_size
    group_count = lax.axis_size("dp")
    w_all = lax.all_gather(w_blocks, "dp", axis=1, tiled=True)[0]
    ids_all = lax.all_gather(block_ids, "dp", axis=1, tiled=True)[0]
    counts_all = lax.all_gather(counts, "dp", axis=1, tiled=True)[0]
    hidden, partial, gg = local_pass(inputs, grad_hidden, w_all, ids_all, counts_all,
                                     capacity, col_blocks)
    grad_inputs = lax.psum_scatter(partial, "tensor", scatter_dimension=1, tiled=True)
    summed = lax.psum_scatter(gg, "dp", scatter_dimension=0, tiled=True).astype(jnp.float32)
    grad_scale = 1.0 / math.sqrt(tok_rows * group_count)
    grad_blocks = (summed * grad_scale).astype(jnp.bfloat16)[None]
    return (hidden, grad_inputs, grad_blocks)


def solution(mesh):
    in_specs = (
        P("dp", None),
        P("dp", "tensor"),
        P("tensor", "dp", None, None),
        P("tensor", "dp"),
        P("tensor", "dp"),
    )
    out_specs = (P("dp", "tensor"), P("dp", "tensor"), P("tensor", "dp", None, None))
    return jax.shard_map(
        per_device, mesh=mesh, in_specs=in_specs, out_specs=out_specs, check_vma=False
    )
```

```python
import functools
import math

import jax
import jax.numpy as jnp
from jax import lax
from jax.experimental import pallas as pl
from jax.experimental.pallas import tpu as pltpu
from jax.sharding import PartitionSpec as P

GELU_C = 0.7978845608028654
GELU_A = 0.044715
ID_SPLIT = 32
META_ROWS = 8


def gelu_value(values):
    inner_arg = GELU_C * (values + GELU_A * values * values * values)
    return 0.5 * values * (1.0 + jnp.tanh(inner_arg))


def gelu_slope(values):
    inner_arg = GELU_C * (values + GELU_A * values * values * values)
    tanh_value = jnp.tanh(inner_arg)
    return 0.5 * (1.0 + tanh_value) + 0.5 * values * (1.0 - tanh_value * tanh_value) * GELU_C * (
        1.0 + 3.0 * GELU_A * values * values
    )


def slot_info(capacity, col_blocks, blk, ids_ref, counts_ref, s):
    live = (s % capacity) < counts_ref[s // capacity]
    bid = ids_ref[s]
    row = pl.multiple_of((bid // col_blocks) * blk, blk)
    col = pl.multiple_of((bid % col_blocks) * blk, blk)
    return live, row, col


def forward_kernel(capacity, col_blocks, ids_ref, counts_ref, x_ref, xt_ref, gh_ref, w_ref,
                   hidden_ref, gp_ref, gg_ref, pre_ref):
    owners = w_ref.shape[0]
    blk = w_ref.shape[-1]
    slots = owners * capacity
    info = functools.partial(slot_info, capacity, col_blocks, blk, ids_ref, counts_ref)

    pre_ref[...] = jnp.zeros_like(pre_ref)

    def fwd(s, carry):
        live, row, col = info(s)

        @pl.when(live)
        def _():
            w = w_ref[s // capacity, pl.ds(pl.multiple_of((s % capacity) * blk, blk), blk), :]
            xr = x_ref[:, pl.ds(row, blk)]
            pre_ref[:, pl.ds(col, blk)] += jnp.dot(xr, w, preferred_element_type=jnp.float32)

        return carry

    lax.fori_loop(0, slots, fwd, 0)

    pre = pre_ref[...]
    hidden_ref[...] = gelu_value(pre).astype(hidden_ref.dtype)
    gp_ref[...] = (gh_ref[...].astype(jnp.float32) * gelu_slope(pre)).astype(gp_ref.dtype)

    def grads(s, carry):
        live, row, col = info(s)

        @pl.when(live)
        def _():
            g = gp_ref[:, pl.ds(col, blk)]
            xt = xt_ref[pl.ds(row, blk), :]
            gg_ref[s] = jnp.dot(xt, g, preferred_element_type=jnp.float32).astype(gg_ref.dtype)

        @pl.when(jnp.logical_not(live))
        def _():
            gg_ref[s] = jnp.zeros((blk, blk), gg_ref.dtype)

        return carry

    lax.fori_loop(0, slots, grads, 0)


def backward_kernel(capacity, col_blocks, ids_ref, counts_ref, gp_ref, w_ref, partial_ref, acc_ref):
    owners = w_ref.shape[0]
    blk = w_ref.shape[-1]
    slots = owners * capacity
    info = functools.partial(slot_info, capacity, col_blocks, blk, ids_ref, counts_ref)
    acc_ref[...] = jnp.zeros_like(acc_ref)

    def bwd(s, carry):
        live, row, col = info(s)

        @pl.when(live)
        def _():
            w = w_ref[s // capacity, pl.ds(pl.multiple_of((s % capacity) * blk, blk), blk), :]
            g = gp_ref[:, pl.ds(col, blk)]
            acc_ref[:, pl.ds(row, blk)] += lax.dot_general(
                g, w, (((1,), (1,)), ((), ())), preferred_element_type=jnp.float32)

        return carry

    lax.fori_loop(0, slots, bwd, 0)
    parts, _, piece = partial_ref.shape
    for k in range(parts):
        partial_ref[k] = acc_ref[:, k * piece:(k + 1) * piece].astype(partial_ref.dtype)


def forward_pass(x, xt, gh, w, ids, counts, capacity, col_blocks):
    tok, width = x.shape
    ff = gh.shape[1]
    owners, _, blk = w.shape
    slots = owners * capacity
    smem = pl.BlockSpec(memory_space=pltpu.SMEM)
    vmem = pl.BlockSpec(memory_space=pltpu.VMEM)
    return pl.pallas_call(
        functools.partial(forward_kernel, capacity, col_blocks),
        out_shape=(
            jax.ShapeDtypeStruct((tok, ff), jnp.bfloat16),
            jax.ShapeDtypeStruct((tok, ff), jnp.bfloat16),
            jax.ShapeDtypeStruct((slots, blk, blk), jnp.bfloat16),
        ),
        in_specs=[smem, smem, vmem, vmem, vmem, vmem],
        out_specs=(vmem, vmem, vmem),
        scratch_shapes=[pltpu.VMEM((tok, ff), jnp.float32)],
        compiler_params=pltpu.CompilerParams(vmem_limit_bytes=60 * 1024 * 1024),
        cost_estimate=pl.CostEstimate(
            flops=2 * 2 * tok * blk * blk * (slots // 2), transcendentals=2 * tok * ff,
            bytes_accessed=2 * (2 * x.size + 3 * gh.size + w.size + slots * blk * blk)),
    )(ids, counts, x, xt, gh, w)


def backward_pass(gp, w, ids, counts, capacity, col_blocks, width, parts):
    tok, ff = gp.shape
    owners, _, blk = w.shape
    slots = owners * capacity
    smem = pl.BlockSpec(memory_space=pltpu.SMEM)
    vmem = pl.BlockSpec(memory_space=pltpu.VMEM)
    return pl.pallas_call(
        functools.partial(backward_kernel, capacity, col_blocks),
        out_shape=jax.ShapeDtypeStruct((parts, tok, width // parts), jnp.bfloat16),
        in_specs=[smem, smem, vmem, vmem],
        out_specs=vmem,
        scratch_shapes=[pltpu.VMEM((tok, width), jnp.float32)],
        compiler_params=pltpu.CompilerParams(vmem_limit_bytes=60 * 1024 * 1024),
        cost_estimate=pl.CostEstimate(
            flops=2 * tok * blk * blk * (slots // 2), transcendentals=0,
            bytes_accessed=2 * (gp.size + w.size + tok * width)),
    )(ids, counts, gp, w)


def per_device(inputs, grad_hidden, w_blocks, block_ids, counts):
    tok_rows, model_width = inputs.shape
    block_size = w_blocks.shape[-1]
    capacity = w_blocks.shape[1]
    col_blocks = grad_hidden.shape[1] // block_size
    group_count = lax.axis_size("dp")
    parts = lax.axis_size("tensor")
    ids_row = block_ids[0]
    meta = jnp.zeros((META_ROWS, block_size), jnp.float32)
    meta = meta.at[0, :capacity].set((ids_row // ID_SPLIT).astype(jnp.float32))
    meta = meta.at[1, :capacity].set((ids_row % ID_SPLIT).astype(jnp.float32))
    meta = meta.at[2, 0].set(counts[0, 0].astype(jnp.float32))
    packed = jnp.concatenate(
        [w_blocks.reshape(capacity * block_size, block_size), meta.astype(jnp.bfloat16)], axis=0)
    gathered = lax.all_gather(packed[None], "dp", axis=0, tiled=True)
    meta_all = gathered[:, capacity * block_size:, :].astype(jnp.float32).astype(jnp.int32)
    ids_all = (meta_all[:, 0, :capacity] * ID_SPLIT + meta_all[:, 1, :capacity]).reshape(-1)
    counts_all = meta_all[:, 2, 0]
    hidden, gp, gg = forward_pass(inputs, inputs.T, grad_hidden, gathered, ids_all, counts_all,
                                  capacity, col_blocks)
    summed = lax.psum_scatter(gg, "dp", scatter_dimension=0, tiled=True).astype(jnp.float32)
    partial = backward_pass(gp, gathered, ids_all, counts_all, capacity, col_blocks,
                            model_width, parts)
    grad_inputs = lax.psum_scatter(partial, "tensor", scatter_dimension=0, tiled=True)[0]
    grad_scale = 1.0 / math.sqrt(tok_rows * group_count)
    grad_blocks = (summed * grad_scale).astype(jnp.bfloat16)[None]
    return (hidden, grad_inputs, grad_blocks)


def solution(mesh):
    in_specs = (
        P("dp", None),
        P("dp", "tensor"),
        P("tensor", "dp", None, None),
        P("tensor", "dp"),
        P("tensor", "dp"),
    )
    out_specs = (P("dp", "tensor"), P("dp", "tensor"), P("tensor", "dp", None, None))
    return jax.shard_map(
        per_device, mesh=mesh, in_specs=in_specs, out_specs=out_specs, check_vma=False
    )
```
